768 devices in a mesh: lon: 8 (over y_lo, core), lat: 96 (over x, y_hi, z).
Axes of the slice: x: 4, y: 8 (y_hi: 2, y_lo: 4; y = y_hi * 4 + y_lo), z: 12, core: 2. Of those that a mesh axis runs over, the one named last changes fastest.
Arguments:
- forcing: float32 [8, 2304, 4096], P(None, 'lat', 'lon'), may hold values from -6 to 6
- kappa_lon: float32 [8, 2304, 4096], P(None, 'lat', 'lon'), may hold values from 0.025 to 0.2
- kappa_lat: float32 [8, 2304, 4096], P(None, 'lat', 'lon'), may hold values from 0.025 to 0.2
- shear: float32 [8, 2304, 4096], P(None, 'lat', 'lon'), may hold values from -0.8 to 0.8
- amplitude: float32 [8, 2304, 4096], P(None, 'lat', 'lon'), may hold values from 0.5 to 2
- tile_owner: int32 [2304, 32], P('lat', 'lon'), may hold values from -1 to 7, as said below
Outputs:
- packed: float32 [96, 768, 8, 128], P('lat', 'lon')
The draws below stay inside these ranges and needn't reach their ends.
Inputs may be any that keep to these rules, and one draw needn't show every extreme that they name: `tile_owner`: owners lie in the same device row of lat. From the tiles of one device at most 12 go to one owner, and in every device row one owner receives exactly 12 tiles from each device of that row.
All inputs are finite; a program needn't handle non-finite values.
Results may differ from the reference program's by a relative error of at most 0.00015.
Values sent between devices are 32-bit elements; how exact they have to be, the bound alone decides.
A program may use at most 32 MiB of HBM per device.

```python
import math
import jax
import jax.numpy as jnp
from jax import lax

LEV = 8
ITERS = 6
TW = 128
CLAT = 24
TPL = 4
TPD = 96
MOST = 12
RECV = 96
NLAT = 2304
NLON = 4096
NTL = 32
N_LON = 8
N_LAT = 96


def draw_tile_owner(key, part):
    row_keys = jax.random.split(jax.random.fold_in(key, 11), N_LAT)
    device_keys = jax.random.split(jax.random.fold_in(key, 12), N_LAT * N_LON)
    busiest = jax.vmap(lambda row_key: jax.random.randint(row_key, (), 0, N_LON))(row_keys)
    busiest_all = jnp.repeat(busiest, N_LON)

    def device_draw(device_key, chosen):
        count_key, shuffle_key = jax.random.split(device_key)
        counts = jax.random.randint(count_key, (N_LON,), MOST // 2, MOST + 1)
        counts = jnp.where(jnp.arange(N_LON) == chosen, MOST, counts)
        bounds = jnp.cumsum(counts)
        shuffle = jax.random.permutation(shuffle_key, TPD)
        position = jnp.arange(TPD)
        labels = jnp.sum((position[:, None] >= bounds[None, :]).astype(jnp.int32), axis=1)
        labels = jnp.where(labels >= N_LON, -1, labels).astype(jnp.int32)
        return jnp.zeros((TPD,), jnp.int32).at[shuffle].set(labels)
    blocks = jax.vmap(device_draw)(device_keys, busiest_all)
    blocks = blocks.reshape(N_LAT, N_LON, CLAT, TPL).transpose(0, 2, 1, 3)
    return blocks.reshape(NLAT, NTL)


def steps_of(key, extent, pieces, smallest, top_value):
    loudness = 1.0
    for dim, blocks in pieces:
        heights = jax.random.uniform(jax.random.fold_in(jax.random.fold_in(key, 6), dim), (blocks,), jnp.float32, smallest / len(pieces), top_value / len(pieces))
        loudness = loudness * jnp.repeat(jnp.exp(heights), extent[dim] // blocks).reshape((-1,) + (1,) * (len(extent) - 1 - dim))
    return loudness


def centred(own_key, dims, spread, limit, pieces=(), kind=jnp.bfloat16):
    factor_of = steps_of(own_key, dims, pieces, -0.22, 0.18) if pieces else 1.0
    values = jax.random.normal(own_key, dims, jnp.float32) * spread * factor_of
    return jnp.minimum(jnp.maximum(values, -limit), limit).astype(kind)


def setup_inputs(seed: int = 0) -> dict:
    arg_keys = jax.random.split(jax.random.key(seed), 7)
    forcing = centred(arg_keys[0], (LEV, NLAT, NLON), 1.0, 6.0, ((1, 96), (2, 8)), jnp.float32)
    kappa_lon = jnp.clip(jnp.exp(math.log(0.2) - 2.0794415 * jax.random.uniform(arg_keys[1], (LEV, NLAT, NLON), jnp.float32) ** steps_of(arg_keys[1], (LEV, NLAT, NLON), ((1, 96), (2, 8)), -0.2, 0.2)), 0.025, 0.2)
    kappa_lat = jnp.clip(jnp.exp(math.log(0.2) - 2.0794415 * jax.random.uniform(arg_keys[2], (LEV, NLAT, NLON), jnp.float32) ** steps_of(arg_keys[2], (LEV, NLAT, NLON), ((1, 96), (2, 8)), -0.2, 0.2)), 0.025, 0.2)
    shear = jnp.clip(jax.random.uniform(arg_keys[3], (LEV, NLAT, NLON), jnp.float32, -0.8, 0.8) * steps_of(arg_keys[3], (LEV, NLAT, NLON), ((1, 96), (2, 8)), -0.4, 0.0), -0.8, 0.8)
    amplitude = jnp.clip(jnp.exp(math.log(2.0) - 1.3862944 * jax.random.uniform(arg_keys[4], (LEV, NLAT, NLON), jnp.float32) ** steps_of(arg_keys[4], (LEV, NLAT, NLON), ((1, 96), (2, 8)), -0.2, 0.2)), 0.5, 2.0)
    tile_owner = draw_tile_owner(jax.random.fold_in(arg_keys[6], 71), 0)
    return {"forcing": forcing, "kappa_lon": kappa_lon, "kappa_lat": kappa_lat, "shear": shear, "amplitude": amplitude, "tile_owner": tile_owner}


def diffuse(state_field, kappa_lon, kappa_lat, cross_term, ocean_mask):
    centre = state_field[:, 1:-1, 1:-1]
    east_cell = state_field[:, 1:-1, 2:]
    west_cell = state_field[:, 1:-1, :-2]
    north_cell = state_field[:, 2:, 1:-1]
    south_cell = state_field[:, :-2, 1:-1]
    upper_east = state_field[:, 2:, 2:]
    upper_west = state_field[:, 2:, :-2]
    lower_east = state_field[:, :-2, 2:]
    lower_west = state_field[:, :-2, :-2]
    change = kappa_lon * (east_cell + west_cell - 2.0 * centre)
    change = change + kappa_lat * (north_cell + south_cell - 2.0 * centre)
    change = change + cross_term * (upper_east - upper_west - lower_east + lower_west)
    return centre + ocean_mask * change

def extend_full(state_field):
    mirror_row = jnp.flip(state_field[:, -1:, :], axis=2)
    zero_row = jnp.zeros((state_field.shape[0], 1, state_field.shape[2]), jnp.float32)
    extended = jnp.concatenate([zero_row, state_field, mirror_row], axis=1)
    return jnp.concatenate([extended[:, :, -1:], extended, extended[:, :, :1]], axis=2)

def reference(forcing, kappa_lon, kappa_lat, shear, amplitude, tile_owner):
    ocean = (tile_owner >= 0).astype(jnp.float32)
    ocean_mask = jnp.repeat(ocean, TW, axis=1)[None]
    cross_term = 0.5 * shear * jnp.sqrt(kappa_lon * kappa_lat)
    state_field = ocean_mask * forcing
    for sweep_index in range(ITERS):
        state_field = diffuse(extend_full(state_field), kappa_lon, kappa_lat, cross_term, ocean_mask)
    sample = amplitude * state_field
    tile_data = sample.reshape(LEV, N_LAT, CLAT, N_LON, TPL, TW).transpose(1, 3, 2, 4, 0, 5)
    tile_data = tile_data.reshape(N_LAT, N_LON * TPD, LEV, TW)
    owner_grid = tile_owner.reshape(N_LAT, CLAT, N_LON, TPL).transpose(0, 2, 1, 3).reshape(N_LAT, N_LON, TPD)
    owners_range = jnp.arange(N_LON, dtype=jnp.int32)
    onehot = (owner_grid[..., None] == owners_range[None, None, None, :]).astype(jnp.int32)
    rank_slot = lax.optimization_barrier(jnp.sum((jnp.cumsum(onehot, axis=2) - 1) * onehot, axis=3))
    source_index = owners_range[None, :, None]
    slot_index = owner_grid * RECV + source_index * MOST + rank_slot
    slot_index = jnp.where(owner_grid >= 0, slot_index, N_LON * RECV).astype(jnp.int32)
    slot_index = slot_index.reshape(N_LAT, N_LON * TPD)
    row_index = jnp.broadcast_to(jnp.arange(N_LAT, dtype=jnp.int32)[:, None], slot_index.shape)
    packed = jnp.zeros((N_LAT, N_LON * RECV, LEV, TW), jnp.float32)
    packed = packed.at[row_index, slot_index].set(tile_data, mode='drop')
    return packed
```

```python
import functools

import jax
import jax.numpy as jnp
from jax import lax
from jax.experimental import pallas as pl
from jax.experimental.pallas import tpu as pltpu
from jax.sharding import PartitionSpec as P

ITERS = 6
LEVELS = 8
WIDTH = 128
ROWS = 24
TILES = 4
RING = 5
GROUP = 8
TOTAL = ROWS + 2 * GROUP
OWNERS = 8
MOST = 12
PIECES = 2
MESH = pl.DeviceIdType.MESH


def lanes(shape=(LEVELS, WIDTH)):
    return lax.broadcasted_iota(jnp.int32, shape, len(shape) - 1)


def neighbours(row, lane):
    left = [pltpu.roll(v, WIDTH - 1, axis=1) for v in row]
    right = [pltpu.roll(v, 1, axis=1) for v in row]
    east = [jnp.where(lane == WIDTH - 1, left[(q + 1) % RING], left[q]) for q in range(RING)]
    west = [jnp.where(lane == 0, right[(q - 1) % RING], right[q]) for q in range(RING)]
    both = [e + w for e, w in zip(east, west)]
    slope = [e - w for e, w in zip(east, west)]
    return both, slope


def updated(coef, r, south, centre, north, lane_terms):
    south_slope, both, north_slope = lane_terms
    new = []
    for q in range(RING):
        twice = 2.0 * centre[q]
        change = coef[0, r, q] * (both[q] - twice)
        change = change + coef[1, r, q] * (north[q] + south[q] - twice)
        change = change + coef[2, r, q] * (north_slope[q] - south_slope[q])
        new.append(centre[q] + change)
    return new


def row_of(state, plane, r):
    return [state[plane, r, q] for q in range(RING)]


def sweep(state, coef, src, dst, low, count, below=None, above=None):
    lane = lanes()
    south = row_of(state, src, low - 1) if below is None else below
    centre = row_of(state, src, low)
    _, south_slope = neighbours(south, lane)
    both, slope = neighbours(centre, lane)

    def step(r, north, carry):
        south, south_slope, centre, both, slope = carry
        north_both, north_slope = neighbours(north, lane)
        new = updated(coef, r, south, centre, north, (south_slope, both, north_slope))
        for q in range(RING):
            state[dst, r, q] = new[q]
        return centre, slope, north, north_both, north_slope

    def body(i, carry):
        r = low + i
        return step(r, row_of(state, src, r + 1), carry)

    carry = (south, south_slope, centre, both, slope)
    if above is None:
        lax.fori_loop(0, count, body, carry)
    else:
        carry = lax.fori_loop(0, count - 1, body, carry)
        step(low + count - 1, above, carry)


def kernel(
    forcing, kappa_lon, kappa_lat, shear, amplitude, owner, out,
    raw, state, coef, scale, saved, lon_send, lon_recv, lat_recv, packed, index_v, index_s,
    load_sem, lon_ssem, lon_rsem, lat_ssem, lat_rsem, out_ssem, out_rsem, own_sem, index_sem,
):
    s = lax.axis_index("lon")
    a = lax.axis_index("lat")
    n_lon = lax.axis_size("lon")
    n_lat = lax.axis_size("lat")
    fold = a // (n_lat - 1)
    has_south = a > 0
    north_lon = s + fold * (n_lon - 1 - 2 * s)
    north_lat = a + 1 - fold
    east = lax.rem(s + 1, n_lon)
    west = lax.rem(s + n_lon - 1, n_lon)

    barrier = pltpu.get_barrier_semaphore()
    for d in range(1, OWNERS):
        pl.semaphore_signal(barrier, inc=1, device_id=(lax.rem(s + d, n_lon), a), device_id_type=MESH)

    @pl.when(fold == 0)
    def _():
        pl.semaphore_signal(barrier, inc=1, device_id=(s, a + 1), device_id_type=MESH)

    @pl.when(has_south)
    def _():
        pl.semaphore_signal(barrier, inc=1, device_id=(s, a - 1), device_id_type=MESH)

    loads = [
        pltpu.make_async_copy(ref.at[:, pl.ds(q * WIDTH, WIDTH)], raw.at[i, q], load_sem.at[i, q])
        for i, ref in enumerate((forcing, kappa_lon, kappa_lat, shear, amplitude))
        for q in range(TILES)
    ]
    for load in loads:
        load.start()
    for load in loads:
        load.wait()

    lane = lanes()

    def prepare(r, _):
        for q in range(TILES):
            rows = pl.ds(r, LEVELS, ROWS)
            sea = (owner[r, q] >= 0).astype(jnp.float32)
            k_lon = raw[1, q, rows]
            k_lat = raw[2, q, rows]
            cross = 0.5 * raw[3, q, rows] * jnp.sqrt(k_lon * k_lat)
            state[0, GROUP + r, q] = sea * raw[0, q, rows]
            coef[0, GROUP + r, q] = sea * k_lon
            coef[1, GROUP + r, q] = sea * k_lat
            coef[2, GROUP + r, q] = sea * cross
            scale[r, q] = raw[4, q, rows]
        return 0

    lax.fori_loop(0, ROWS, prepare, 0)

    def piece(kind, r, q):
        return state[0, r, q] if kind == 0 else coef[kind - 1, r, q]

    per_vector = WIDTH // GROUP

    def pack_group(g, _):
        for v in range(PIECES):
            to_west = jnp.zeros((LEVELS, WIDTH), jnp.float32)
            to_east = jnp.zeros((LEVELS, WIDTH), jnp.float32)
            for j in range(per_vector):
                rr, kind = divmod(v * per_vector + j, 4)
                r = GROUP + g * GROUP + rr
                here = lane // GROUP == j
                first, last = piece(kind, r, 0), piece(kind, r, TILES - 1)
                if j:
                    first = pltpu.roll(first, GROUP * j, axis=1)
                if j < per_vector - 1:
                    last = pltpu.roll(last, GROUP * (j + 1), axis=1)
                to_west = jnp.where(here, first, to_west)
                to_east = jnp.where(here, last, to_east)
            lon_send[0, g, v] = to_west
            lon_send[1, g, v] = to_east
        return 0

    lax.fori_loop(0, ROWS // GROUP, pack_group, 0)

    def unpack(buf, g, base):
        for v in range(PIECES):
            from_east, from_west = buf[g, 0, v], buf[g, 1, v]
            for j in range(per_vector):
                rr, kind = divmod(v * per_vector + j, 4)
                after = from_east if j == 0 else pltpu.roll(from_east, WIDTH - GROUP * j, axis=1)
                before = from_west if j == per_vector - 1 else pltpu.roll(from_west, WIDTH - GROUP * (j + 1), axis=1)
                ends = jnp.where(lane < ITERS, after, jnp.where(lane >= WIDTH - ITERS, before, 0.0))
                if kind == 0:
                    state[0, base + rr, TILES] = ends
                else:
                    coef[kind - 1, base + rr, TILES] = ends

    def spread(t, vec):
        return jnp.where(lane == t, owner[t // TILES, lax.rem(t, TILES)], vec)

    owner_vec = lax.fori_loop(0, ROWS * TILES, spread, jnp.full((OWNERS, WIDTH), -1, jnp.int32))
    mine = owner_vec == lax.broadcasted_iota(jnp.int32, (OWNERS, WIDTH), 0)
    rank = mine.astype(jnp.int32)
    for shift in (1, 2, 4, 8, 16, 32, 64):
        rank = rank + jnp.where(lane >= shift, pltpu.roll(rank, shift, axis=1), 0)
    index = jnp.full((OWNERS, WIDTH), -1, jnp.int32)
    for k in range(MOST):
        place = jnp.sum(jnp.where(mine & (rank == k + 1), lane + 1, 0), axis=1, keepdims=True) - 1
        index = jnp.where(lane == k, place, index)
    index_v[...] = index
    index_copy = pltpu.make_async_copy(index_v, index_s, index_sem)
    index_copy.start()

    pl.semaphore_wait(barrier, OWNERS - 1 + (1 - fold) + (a + n_lat - 1) // n_lat)

    def remote(src, dst, ssem, rsem, lon, lat):
        return pltpu.make_async_remote_copy(
            src_ref=src, dst_ref=dst, send_sem=ssem, recv_sem=rsem, device_id=(lon, lat), device_id_type=MESH
        )

    main = pl.ds(0, TILES)
    up = fold * (ROWS + GROUP)
    top = GROUP + ROWS
    to_west = remote(lon_send.at[0], lon_recv.at[:, 0], lon_ssem.at[0], lon_rsem.at[0], west, a)
    to_east = remote(lon_send.at[1], lon_recv.at[:, 1], lon_ssem.at[1], lon_rsem.at[1], east, a)
    northward = [
        remote(
            state.at[0, pl.ds(top - ITERS, ITERS), main], state.at[0, pl.ds(up + GROUP - ITERS, ITERS), main],
            lat_ssem.at[0], lat_rsem.at[fold, 0], north_lon, north_lat,
        ),
        remote(
            coef.at[:, pl.ds(top - ITERS + 1, ITERS - 1), main], coef.at[:, pl.ds(up + GROUP - ITERS + 1, ITERS - 1), main],
            lat_ssem.at[1], lat_rsem.at[fold, 1], north_lon, north_lat,
        ),
        remote(lon_recv.at[ROWS // GROUP - 1], lat_recv.at[fold], lat_ssem.at[2], lat_rsem.at[fold, 2], north_lon, north_lat),
    ]
    south_lat = lax.rem(a + n_lat - 1, n_lat)
    southward = [
        remote(
            state.at[0, pl.ds(GROUP, ITERS), main], state.at[0, pl.ds(top, ITERS), main],
            lat_ssem.at[3], lat_rsem.at[1, 0], s, south_lat,
        ),
        remote(
            coef.at[:, pl.ds(GROUP, ITERS - 1), main], coef.at[:, pl.ds(top, ITERS - 1), main],
            lat_ssem.at[4], lat_rsem.at[1, 1], s, south_lat,
        ),
        remote(lon_recv.at[0], lat_recv.at[1], lat_ssem.at[5], lat_rsem.at[1, 2], s, south_lat),
    ]

    to_west.start()
    to_east.start()
    northward[0].start()
    northward[1].start()

    @pl.when(has_south)
    def _():
        southward[0].start()
        southward[1].start()

    to_west.wait_recv()
    to_east.wait_recv()
    northward[2].start()

    @pl.when(has_south)
    def _():
        southward[2].start()

    def unpack_own(g, _):
        unpack(lon_recv, g, GROUP + g * GROUP)
        return 0

    lax.fori_loop(0, ROWS // GROUP, unpack_own, 0)

    for turn in range(1, ITERS + 1):
        src = 0 if turn == 1 else 1
        for q in range(RING):
            saved[0, turn - 1, q] = state[src, GROUP + turn, q]
            saved[1, turn - 1, q] = state[src, top - 1 - turn, q]
        sweep(state, coef, src, 1, GROUP + turn, ROWS - 2 * turn)

    @pl.when(has_south)
    def _():
        for i in range(3):
            remote(
                (state.at[0, pl.ds(top - ITERS, ITERS), main], coef.at[:, pl.ds(top - ITERS + 1, ITERS - 1), main], lon_recv.at[0])[i],
                (
                    state.at[0, pl.ds(GROUP - ITERS, ITERS), main],
                    coef.at[:, pl.ds(GROUP - ITERS + 1, ITERS - 1), main],
                    lat_recv.at[0],
                )[i],
                lat_ssem.at[i], lat_rsem.at[0, i], north_lon, north_lat,
            ).wait_recv()
        unpack(lat_recv, 0, 0)

    @pl.when(a == 0)
    def _():
        zero = jnp.zeros((LEVELS, WIDTH), jnp.float32)

        def clear(r, _):
            for q in range(RING):
                state[0, r, q] = zero
                for kind in range(3):
                    coef[kind, r, q] = zero
            return 0

        lax.fori_loop(0, GROUP, clear, 0)

    def south_turn(turn, _):
        src = (turn + ITERS - 2) // ITERS
        above = [saved[0, turn - 1, q] for q in range(RING)]
        sweep(state, coef, src, 1, GROUP - ITERS + turn, ITERS, above=above)
        return 0

    lax.fori_loop(1, ITERS + 1, south_turn, 0)

    for copy in southward:
        copy.wait_recv()
    unpack(lat_recv, 1, top)

    @pl.when(fold == 1)
    def _():
        mirror = WIDTH - 1 - lane

        def flipped(value):
            return jnp.take_along_axis(value, mirror, axis=1)

        def swap(m, _):
            low, high = top + m, top + GROUP - 1 - m
            for get, put in [
                (lambda r, q: state[0, r, q], 0),
                (lambda r, q: coef[0, r, q], 1),
                (lambda r, q: coef[1, r, q], 2),
                (lambda r, q: coef[2, r, q], 3),
            ]:
                old_low = [get(low, q) for q in range(RING)]
                old_high = [get(high, q) for q in range(RING)]
                for q in range(RING):
                    p = TILES - 1 - q if q < TILES else q
                    for r, value in ((low, old_high[p]), (high, old_low[p])):
                        if put == 0:
                            state[0, r, q] = flipped(value)
                        else:
                            coef[put - 1, r, q] = flipped(value)
            return 0

        lax.fori_loop(0, GROUP // 2, swap, 0)

    def north_turn(turn, _):
        src = (turn + ITERS - 2) // ITERS
        below = [saved[1, turn - 1, q] for q in range(RING)]
        sweep(state, coef, src, 1, top - turn, ITERS, below=below)
        return 0

    lax.fori_loop(1, ITERS + 1, north_turn, 0)

    index_copy.wait()

    def fill(o):
        for k in range(MOST):
            t = index_s[o, k]
            r = jnp.maximum(t, 0) // TILES
            q = jnp.maximum(t, 0) - r * TILES
            tile = scale[r, q] * state[1, GROUP + r, q]
            packed[o * MOST + k] = jnp.where(t >= 0, tile, 0.0)

    def to_owner(o, d):
        block = pl.ds(o * MOST, MOST)
        slot = pl.ds(s * MOST, MOST)
        return remote(packed.at[block], out.at[0, slot], out_ssem.at[d], out_rsem.at[d], o, a)

    def give(d, _):
        o = lax.rem(s + d, n_lon)
        fill(o)
        to_owner(o, d).start()
        return 0

    lax.fori_loop(1, OWNERS, give, 0)
    fill(s)
    own = pltpu.make_async_copy(packed.at[pl.ds(s * MOST, MOST)], out.at[0, pl.ds(s * MOST, MOST)], own_sem)
    own.start()
    to_west.wait_send()
    to_east.wait_send()
    for copy in northward:
        copy.wait_send()

    @pl.when(has_south)
    def _():
        for copy in southward:
            copy.wait_send()

    own.wait()

    def finish(d, _):
        to_owner(lax.rem(s + d, n_lon), d).wait()
        return 0

    lax.fori_loop(1, OWNERS, finish, 0)


def per_device(forcing, kappa_lon, kappa_lat, shear, amplitude, tile_owner):
    flat = [v.reshape(LEVELS * ROWS, TILES * WIDTH) for v in (forcing, kappa_lon, kappa_lat, shear, amplitude)]
    vmem = functools.partial(pltpu.VMEM, dtype=jnp.float32)
    dma = pltpu.SemaphoreType.DMA
    return pl.pallas_call(
        kernel,
        out_shape=jax.ShapeDtypeStruct((1, OWNERS * MOST, LEVELS, WIDTH), jnp.float32),
        in_specs=[pl.BlockSpec(memory_space=pl.ANY)] * 5 + [pl.BlockSpec(memory_space=pltpu.SMEM)],
        out_specs=pl.BlockSpec(memory_space=pl.ANY),
        scratch_shapes=[
            vmem((5, TILES, LEVELS * ROWS, WIDTH)),
            vmem((2, TOTAL, RING, LEVELS, WIDTH)),
            vmem((3, TOTAL, RING, LEVELS, WIDTH)),
            vmem((ROWS, TILES, LEVELS, WIDTH)),
            vmem((2, ITERS, RING, LEVELS, WIDTH)),
            vmem((2, ROWS // GROUP, PIECES, LEVELS, WIDTH)),
            vmem((ROWS // GROUP, 2, PIECES, LEVELS, WIDTH)),
            vmem((2, 2, PIECES, LEVELS, WIDTH)),
            vmem((OWNERS * MOST, LEVELS, WIDTH)),
            pltpu.VMEM((OWNERS, WIDTH), jnp.int32),
            pltpu.SMEM((OWNERS, WIDTH), jnp.int32),
            dma((5, TILES)),
            dma((2,)),
            dma((2,)),
            dma((6,)),
            dma((2, 3)),
            dma((OWNERS,)),
            dma((OWNERS,)),
            dma,
            dma,
        ],
        compiler_params=pltpu.CompilerParams(collective_id=0, has_side_effects=True),
    )(*flat, tile_owner)


def solution(mesh):
    return jax.shard_map(
        per_device,
        mesh=mesh,
        in_specs=(P(None, "lat", "lon"),) * 5 + (P("lat", "lon"),),
        out_specs=P("lat", "lon", None, None),
        check_vma=False,
    )
```

```python
import functools

import jax
import jax.numpy as jnp
from jax import lax
from jax.experimental import pallas as pl
from jax.experimental.pallas import tpu as pltpu
from jax.sharding import PartitionSpec as P

ITERS = 6
LEVELS = 8
WIDTH = 128
ROWS = 24
TILES = 4
RING = 5
GROUP = 8
TOTAL = ROWS + 2 * GROUP
OWNERS = 8
MOST = 12
CHIPS_Z = 12
PIECES = 2
MESH = pl.DeviceIdType.MESH


def lanes(shape=(LEVELS, WIDTH)):
    return lax.broadcasted_iota(jnp.int32, shape, len(shape) - 1)


def neighbours(row, lane):
    left = [pltpu.roll(v, WIDTH - 1, axis=1) for v in row]
    right = [pltpu.roll(v, 1, axis=1) for v in row]
    east = [jnp.where(lane == WIDTH - 1, left[(q + 1) % RING], left[q]) for q in range(RING)]
    west = [jnp.where(lane == 0, right[(q - 1) % RING], right[q]) for q in range(RING)]
    both = [e + w for e, w in zip(east, west)]
    slope = [e - w for e, w in zip(east, west)]
    return both, slope


def updated(field, r, south, centre, north, lane_terms, sign):
    south_slope, both, north_slope = lane_terms
    new = []
    for q in range(RING):
        twice = 2.0 * centre[q]
        change = field[r, 1, q] * (both[q] - twice)
        change = change + field[r, 2, q] * (north[q] + south[q] - twice)
        cross = north_slope[q] - south_slope[q]
        change = change + field[r, 3, q] * (cross if sign is None else sign * cross)
        new.append(centre[q] + change)
    return new


def row_of(field, later, turn, r):
    return [field[r, 0, q] if turn == 0 else later[(turn - 1) % 2, r, q] for q in range(RING)]


def store(later, turn, r, new):
    for q in range(RING):
        later[(turn - 1) % 2, r, q] = new[q]


def sweep(field, later, turn, low, count):
    lane = lanes()
    south = row_of(field, later, turn - 1, low - 1)
    centre = row_of(field, later, turn - 1, low)
    _, south_slope = neighbours(south, lane)
    both, slope = neighbours(centre, lane)

    def body(i, carry):
        south, south_slope, centre, both, slope = carry
        r = low + i
        north = row_of(field, later, turn - 1, r + 1)
        north_both, north_slope = neighbours(north, lane)
        store(later, turn, r, updated(field, r, south, centre, north, (south_slope, both, north_slope), None))
        return centre, slope, north, north_both, north_slope

    lax.fori_loop(0, count, body, (south, south_slope, centre, both, slope), unroll=2)


def diagonal(field, later, start, step, sign):
    lane = lanes()
    outer = row_of(field, later, 0, start - step)
    for turn in range(1, ITERS + 1):
        r = start + step * (turn - 1)
        centre = row_of(field, later, turn - 1, r)
        inner = row_of(field, later, turn - 1, r + step)
        both, _ = neighbours(centre, lane)
        _, inner_slope = neighbours(inner, lane)
        _, outer_slope = neighbours(outer, lane)
        outer = updated(field, r, outer, centre, inner, (outer_slope, both, inner_slope), sign)
        store(later, turn, r, outer)


def kernel(
    forcing, kappa_lon, kappa_lat, shear, amplitude, owner, out,
    raw, field, later, scale, stage, stage_ends, lon_send, lon_recv, lat_recv, packed, owner_s, owner_v, index_v, index_s,
    load_sem, owner_sem, ready_sem, lon_ssem, lon_rsem, north_ssem, relay_ssem, south_ssem, lat_rsem,
    ends_ssem, ends_rsem, stage_rsem, forward_ssem, out_ssem, out_rsem, own_sem, index_sem,
):
    s = lax.axis_index("lon")
    a = lax.axis_index("lat")
    n_lon = lax.axis_size("lon")
    n_lat = lax.axis_size("lat")
    along = lax.rem(a, CHIPS_Z)
    fold = a // (n_lat - 1)
    has_south = (a + n_lat - 1) // n_lat
    wrap = along // (CHIPS_Z - 1) * (1 - fold)
    far = (CHIPS_Z - 1 - along) // (CHIPS_Z - 1) * has_south
    near = has_south - far
    relay_north = ((along == CHIPS_Z - 2) & (a >= CHIPS_Z)).astype(jnp.int32)
    relay_south = ((along == 1) & (a < n_lat - CHIPS_Z)).astype(jnp.int32)
    north_lon = s + fold * (n_lon - 1 - 2 * s)
    north_lat = a + 1 - fold
    east = lax.rem(s + 1, n_lon)
    west = lax.rem(s + n_lon - 1, n_lon)
    groups = ROWS // GROUP
    top = GROUP + ROWS
    lane = lanes()
    fields = (forcing, kappa_lon, kappa_lat, shear, amplitude)

    def load(g, i, q, sem):
        cells = pl.ds(q * WIDTH, WIDTH)
        return pltpu.make_async_copy(fields[i].at[:, pl.ds(g * GROUP, GROUP), cells], raw.at[g, i, q], sem)

    def load_group(g):
        for i in range(4):
            for q in range(TILES):
                load(g, i, q, load_sem.at[g]).start()

    owner_copy = pltpu.make_async_copy(owner, owner_s, owner_sem.at[0])
    owner_copy_v = pltpu.make_async_copy(owner, owner_v, owner_sem.at[1])
    load_group(groups - 1)
    owner_copy.start()

    barrier = pltpu.get_barrier_semaphore()

    def enter(condition, lon, lat):
        @pl.when(condition == 1)
        def _():
            pl.semaphore_signal(barrier, inc=1, device_id=(lon, lat), device_id_type=MESH)

    enter(1 - fold - wrap, s, a + 1)
    enter(has_south, s, a - 1)
    enter(far, s, a + CHIPS_Z - 2)
    enter(relay_north, s, a - (CHIPS_Z - 1))
    enter(relay_south, s, a + CHIPS_Z - 1)
    enter(relay_south, s, a + CHIPS_Z - 2)
    for d in range(1, OWNERS):
        pl.semaphore_signal(barrier, inc=1, device_id=(lax.rem(s + d, n_lon), a), device_id_type=MESH)

    load_group(0)
    load_group(1)
    owner_copy_v.start()
    for g in range(groups):
        for q in range(TILES):
            load(g, 4, q, load_sem.at[groups]).start()

    flat = raw.reshape(groups * 5 * TILES * LEVELS * GROUP, WIDTH)

    def cells_of(g, i, q, rr):
        return flat[pl.ds(((g * 5 + i) * TILES + q) * LEVELS * GROUP + rr, LEVELS, GROUP)]

    def prepare_group(g):
        whole = raw.at[g, pl.ds(0, 4)]
        pltpu.make_async_copy(whole, whole, load_sem.at[g]).wait()

        def prepare(rr, _):
            r = g * GROUP + rr
            for q in range(TILES):
                sea = (owner_s[r, q] >= 0).astype(jnp.float32)
                k_lon = cells_of(g, 1, q, rr)
                k_lat = cells_of(g, 2, q, rr)
                cross = 0.5 * cells_of(g, 3, q, rr) * jnp.sqrt(k_lon * k_lat)
                field[GROUP + r, 0, q] = sea * cells_of(g, 0, q, rr)
                field[GROUP + r, 1, q] = sea * k_lon
                field[GROUP + r, 2, q] = sea * k_lat
                field[GROUP + r, 3, q] = sea * cross
            return 0

        lax.fori_loop(0, GROUP, prepare, 0)

    def remote(src, dst, ssem, rsem, lon, lat):
        return pltpu.make_async_remote_copy(
            src_ref=src, dst_ref=dst, send_sem=ssem, recv_sem=rsem, device_id=(lon, lat), device_id_type=MESH
        )

    def part(ref, place, k, first=0, count=TILES):
        return ref.at[place, pl.ds(0, 4 if k < ITERS else 1), pl.ds(first, count)]

    half = TILES // 2

    def north_copies(k_size, k):
        own = top - k
        plain = remote(
            part(field, own, k_size), part(field, GROUP - k + fold * (top - 1 - GROUP + 2 * k), k_size),
            north_ssem.at[k - 1], lat_rsem.at[fold, 0, k - 1], north_lon, north_lat,
        )
        direct = remote(
            part(field, own, k_size, 0, half), part(field, GROUP - k, k_size, 0, half),
            north_ssem.at[k - 1], lat_rsem.at[0, 0, k - 1], s, north_lat,
        )
        around = remote(
            part(field, own, k_size, half, half), part(stage, k - 1, k_size, half, half),
            relay_ssem.at[k - 1], stage_rsem.at[k - 1], s, lax.rem(a + CHIPS_Z - 1, n_lat),
        )
        return plain, direct, around

    def south_copies(k_size, k):
        own = GROUP + k - 1
        plain = remote(
            part(field, own, k_size), part(field, top + k - 1, k_size),
            south_ssem.at[k - 1], lat_rsem.at[1, 0, k - 1], s, lax.rem(a + n_lat - 1, n_lat),
        )
        around = remote(
            part(field, own, k_size), part(stage, k - 1, k_size),
            south_ssem.at[k - 1], stage_rsem.at[k - 1], s, lax.rem(a + n_lat - (CHIPS_Z - 1), n_lat),
        )
        return plain, around

    def each_row(low, high, act):
        for_size = min(high, ITERS - 1)

        def one(k, _):
            act(1, k)
            return 0

        lax.fori_loop(low, for_size + 1, one, 0)
        if high == ITERS:
            act(ITERS, ITERS)

    def send_north(low, high):
        def act(k_size, k):
            plain, direct, around = north_copies(k_size, k)

            @pl.when(wrap == 0)
            def _():
                plain.start()

            @pl.when(wrap == 1)
            def _():
                direct.start()
                around.start()

        each_row(low, high, act)

    def send_south(low, high):
        def act(k_size, k):
            plain, around = south_copies(k_size, k)

            @pl.when(near == 1)
            def _():
                plain.start()

            @pl.when(far == 1)
            def _():
                around.start()

        each_row(low, high, act)

    ends_north = remote(
        lon_recv.at[groups - 1], lat_recv.at[fold], ends_ssem.at[0], ends_rsem.at[fold], north_lon, north_lat
    )
    ends_south = remote(
        lon_recv.at[0], lat_recv.at[1], ends_ssem.at[1], ends_rsem.at[1], s, lax.rem(a + n_lat - 1, n_lat)
    )
    ends_around = remote(
        lon_recv.at[0], stage_ends, ends_ssem.at[1], ends_rsem.at[2], s, lax.rem(a + n_lat - (CHIPS_Z - 1), n_lat)
    )
    ends_forward = remote(stage_ends, lat_recv.at[1], ends_ssem.at[2], ends_rsem.at[1], s, lax.rem(a + CHIPS_Z - 2, n_lat))
    to_west = remote(lon_send.at[0], lon_recv.at[:, 0], lon_ssem.at[0], lon_rsem.at[0], west, a)
    to_east = remote(lon_send.at[1], lon_recv.at[:, 1], lon_ssem.at[1], lon_rsem.at[1], east, a)
    early = ITERS // 2

    owner_copy.wait()
    prepare_group(groups - 1)
    pl.semaphore_wait(barrier, OWNERS - 1 + (1 - fold) + near + 2 * wrap + far + relay_north)

    @pl.when(wrap == 1)
    def _():
        pl.semaphore_signal(ready_sem, inc=1, device_id=(s, a - (CHIPS_Z - 2)), device_id_type=MESH)

    @pl.when(fold == 0)
    def _():
        send_north(1, early)

    prepare_group(0)

    @pl.when(has_south == 1)
    def _():
        send_south(1, early)

    prepare_group(1)

    per_vector = WIDTH // GROUP

    def pack_group(g, _):
        for v in range(PIECES):
            to_west_v = jnp.zeros((LEVELS, WIDTH), jnp.float32)
            to_east_v = jnp.zeros((LEVELS, WIDTH), jnp.float32)
            for j in range(per_vector):
                rr, kind = divmod(v * per_vector + j, 4)
                r = GROUP + g * GROUP + rr
                here = lane // GROUP == j
                first, last = field[r, kind, 0], field[r, kind, TILES - 1]
                if j:
                    first = pltpu.roll(first, GROUP * j, axis=1)
                if j < per_vector - 1:
                    last = pltpu.roll(last, GROUP * (j + 1), axis=1)
                to_west_v = jnp.where(here, first, to_west_v)
                to_east_v = jnp.where(here, last, to_east_v)
            lon_send[0, g, v] = to_west_v
            lon_send[1, g, v] = to_east_v
        return 0

    lax.fori_loop(0, groups, pack_group, 0)
    to_west.start()
    to_east.start()

    @pl.when(fold == 1)
    def _():
        send_north(1, early)

    def unpack(buf, g, base, step):
        for v in range(PIECES):
            from_east, from_west = buf[g, 0, v], buf[g, 1, v]
            for j in range(per_vector):
                rr, kind = divmod(v * per_vector + j, 4)
                after = from_east if j == 0 else pltpu.roll(from_east, WIDTH - GROUP * j, axis=1)
                before = from_west if j == per_vector - 1 else pltpu.roll(from_west, WIDTH - GROUP * (j + 1), axis=1)
                ends = jnp.where(lane < ITERS, after, jnp.where(lane >= WIDTH - ITERS, before, 0.0))
                field[base + step * rr, kind, TILES] = ends

    amplitudes = raw.at[:, pl.ds(4, 1)]
    pltpu.make_async_copy(amplitudes, amplitudes, load_sem.at[groups]).wait()

    def scale_group(g, _):
        def scale_row(rr, _):
            for q in range(TILES):
                scale[g * GROUP + rr, q] = cells_of(g, 4, q, rr)
            return 0

        return lax.fori_loop(0, GROUP, scale_row, 0)

    lax.fori_loop(0, groups, scale_group, 0)

    owner_copy_v.wait()
    down = lax.broadcasted_iota(jnp.int32, (LEVELS, WIDTH), 0)
    column = lax.rem(lane, TILES)
    carried = jnp.zeros((1, WIDTH), jnp.int32)
    ranks, numbers = [], []
    for g in range(groups):
        rows = owner_v[pl.ds(g * GROUP, GROUP), :]
        spread = jnp.broadcast_to(rows[:, 0:1], (GROUP, WIDTH))
        for q in range(1, TILES):
            spread = jnp.where(column == q, jnp.broadcast_to(rows[:, q : q + 1], (GROUP, WIDTH)), spread)
        mine = (spread == lane // TILES).astype(jnp.int32)
        within = mine + jnp.where(column >= 1, pltpu.roll(mine, 1, axis=1), 0)
        within = within + jnp.where(column >= 2, pltpu.roll(within, 2, axis=1), 0)
        total = mine + jnp.where(column % 2 == 0, pltpu.roll(mine, WIDTH - 1, axis=1), pltpu.roll(mine, 1, axis=1))
        total = total + jnp.where(column < 2, pltpu.roll(total, WIDTH - 2, axis=1), pltpu.roll(total, 2, axis=1))
        upto = total
        for shift in (1, 2, 4):
            upto = upto + jnp.where(down >= shift, pltpu.roll(upto, shift, axis=0), 0)
        ranks.append(jnp.where(mine == 1, carried + upto - total + within, 0))
        numbers.append((g * GROUP + down) * TILES + column + 1)
        carried = carried + jnp.sum(total, axis=0, keepdims=True)
    for k in range(MOST):
        place = jnp.zeros((LEVELS, WIDTH), jnp.int32)
        for g in range(groups):
            place = place + jnp.where(ranks[g] == k + 1, numbers[g], 0)
        place = jnp.sum(place, axis=0, keepdims=True)
        place = place + pltpu.roll(jnp.broadcast_to(place, (LEVELS, WIDTH)), WIDTH - 1, axis=1)
        place = place + pltpu.roll(place, WIDTH - 2, axis=1)
        index_v[k : k + 1, :] = place[0:1, :] - 1
    index_copy = pltpu.make_async_copy(index_v, index_s, index_sem)
    index_copy.start()

    to_west.wait_recv()
    to_east.wait_recv()
    ends_north.start()
    send_north(early + 1, ITERS)

    @pl.when(near == 1)
    def _():
        ends_south.start()

    @pl.when(far == 1)
    def _():
        ends_around.start()

    @pl.when(has_south == 1)
    def _():
        send_south(early + 1, ITERS)

    def unpack_own(g, _):
        unpack(lon_recv, g, GROUP + g * GROUP, 1)
        return 0

    lax.fori_loop(0, groups, unpack_own, 0)

    def relay_copies(k_size, k):
        north = remote(
            part(stage, k - 1, k_size, half, half), part(field, GROUP - k, k_size, half, half),
            forward_ssem.at[k - 1], lat_rsem.at[0, 1, k - 1], s, lax.rem(a + n_lat - (CHIPS_Z - 2), n_lat),
        )
        south = remote(
            part(stage, k - 1, k_size), part(field, top + k - 1, k_size),
            forward_ssem.at[k - 1], lat_rsem.at[1, 0, k - 1], s, lax.rem(a + CHIPS_Z - 2, n_lat),
        )
        return north, south

    for turn in range(1, ITERS + 1):
        sweep(field, later, turn, GROUP + turn, ROWS - 2 * turn)

        @pl.when(relay_north == 1)
        def _():
            north_copies(turn, turn)[2].wait_recv()
            relay_copies(turn, turn)[0].start()

    def clear(r, _):
        zero = jnp.zeros((LEVELS, WIDTH), jnp.float32)
        for kind in range(4):
            for q in range(RING):
                field[r, kind, q] = zero
        return 0

    def mirrored(value):
        return jnp.take_along_axis(value, WIDTH - 1 - lane, axis=1)

    def mirror_ends(i, _):
        for kind in range(4):
            field[top + i, kind, TILES] = mirrored(field[top + i, kind, TILES])
        return 0

    def mirror_row(r):
        for kind in range(4):
            old = [field[r, kind, q] for q in range(TILES)]
            for q in range(TILES):
                field[r, kind, q] = mirrored(old[TILES - 1 - q])

    late = wrap + fold

    def edge(i, _):
        side = lax.rem(i + 1 - late, 2)
        step = 1 - 2 * side
        sign = step.astype(jnp.float32)
        arrives = (side + has_south + 1) // 2
        mirror = side * fold
        halves = (1 - side) * far

        @pl.when(arrives == 1)
        def _():
            remote(
                lon_recv.at[0], lat_recv.at[side], ends_ssem.at[0], ends_rsem.at[side], north_lon, north_lat
            ).wait_recv()
            unpack(lat_recv, side, side * top + mirror * (GROUP - 1), 1 - 2 * mirror)

        @pl.when(mirror == 1)
        def _():
            lax.fori_loop(0, GROUP, mirror_ends, 0)

        @pl.when(arrives == 0)
        def _():
            lax.fori_loop(0, GROUP, clear, 0)

        def arrive(k_size, k):
            def await_row(part_of, first, count):
                place = part(field, GROUP, k_size, first, count)
                remote(
                    place, place, north_ssem.at[k - 1], lat_rsem.at[side, part_of, k - 1], north_lon, north_lat
                ).wait_recv()

            @pl.when(arrives - halves == 1)
            def _():
                await_row(0, 0, TILES)

            @pl.when(halves == 1)
            def _():
                await_row(0, 0, half)
                await_row(1, half, half)

            @pl.when(mirror == 1)
            def _():
                mirror_row(top + k - 1)

        def outward(k, _):
            @pl.when(k < ITERS)
            def _():
                arrive(1, k)

            @pl.when(k == ITERS)
            def _():
                arrive(ITERS, ITERS)

            diagonal(field, later, GROUP + side * (ROWS - 1) + step * (1 - k), step, sign)
            return 0

        lax.fori_loop(1, ITERS + 1, outward, 0)
        return 0

    lax.fori_loop(0, 2, edge, 0)

    @pl.when(relay_south == 1)
    def _():
        pl.semaphore_wait(ready_sem, 1)
        ends_around.wait_recv()
        ends_forward.start()

        def act(k_size, k):
            south_copies(k_size, k)[1].wait_recv()
            relay_copies(k_size, k)[1].start()

        each_row(1, ITERS, act)

    index_copy.wait()

    def fill(o):
        for k in range(MOST):
            t = index_s[k, o * TILES]
            r = jnp.maximum(t, 0) // TILES
            q = jnp.maximum(t, 0) - r * TILES
            tile = scale[r, q] * later[(ITERS - 1) % 2, GROUP + r, q]
            packed[o * MOST + k] = jnp.where(t >= 0, tile, 0.0)

    def to_owner(o, d):
        block = pl.ds(o * MOST, MOST)
        slot = pl.ds(s * MOST, MOST)
        return remote(packed.at[block], out.at[0, slot], out_ssem.at[d], out_rsem.at[d], o, a)

    def give(d, _):
        o = lax.rem(s + d, n_lon)
        fill(o)
        to_owner(o, d).start()
        return 0

    lax.fori_loop(1, OWNERS, give, 0)
    fill(s)
    own = pltpu.make_async_copy(packed.at[pl.ds(s * MOST, MOST)], out.at[0, pl.ds(s * MOST, MOST)], own_sem)
    own.start()
    to_west.wait_send()
    to_east.wait_send()
    ends_north.wait_send()

    def drain(k_size, k):
        plain, direct, around = north_copies(k_size, k)

        @pl.when(wrap == 0)
        def _():
            plain.wait_send()

        @pl.when(wrap == 1)
        def _():
            direct.wait_send()
            around.wait_send()

        @pl.when(has_south == 1)
        def _():
            south_copies(k_size, k)[0].wait_send()

        @pl.when(relay_north == 1)
        def _():
            relay_copies(k_size, k)[0].wait_send()

        @pl.when(relay_south == 1)
        def _():
            relay_copies(k_size, k)[1].wait_send()

    each_row(1, ITERS, drain)

    @pl.when(has_south == 1)
    def _():
        ends_south.wait_send()

    @pl.when(relay_south == 1)
    def _():
        ends_forward.wait_send()

    own.wait()

    def finish(d, _):
        to_owner(lax.rem(s + d, n_lon), d).wait()
        return 0

    lax.fori_loop(1, OWNERS, finish, 0)


def per_device(forcing, kappa_lon, kappa_lat, shear, amplitude, tile_owner):
    vmem = functools.partial(pltpu.VMEM, dtype=jnp.float32)
    dma = pltpu.SemaphoreType.DMA
    return pl.pallas_call(
        kernel,
        out_shape=jax.ShapeDtypeStruct((1, OWNERS * MOST, LEVELS, WIDTH), jnp.float32),
        in_specs=[pl.BlockSpec(memory_space=pl.ANY)] * 6,
        out_specs=pl.BlockSpec(memory_space=pl.ANY),
        scratch_shapes=[
            vmem((ROWS // GROUP, 5, TILES, LEVELS, GROUP, WIDTH)),
            vmem((TOTAL, 4, RING, LEVELS, WIDTH)),
            vmem((2, TOTAL, RING, LEVELS, WIDTH)),
            vmem((ROWS, TILES, LEVELS, WIDTH)),
            vmem((ITERS, 4, TILES, LEVELS, WIDTH)),
            vmem((2, PIECES, LEVELS, WIDTH)),
            vmem((2, ROWS // GROUP, PIECES, LEVELS, WIDTH)),
            vmem((ROWS // GROUP, 2, PIECES, LEVELS, WIDTH)),
            vmem((2, 2, PIECES, LEVELS, WIDTH)),
            vmem((OWNERS * MOST, LEVELS, WIDTH)),
            pltpu.SMEM((ROWS, TILES), jnp.int32),
            pltpu.VMEM((ROWS, TILES), jnp.int32),
            pltpu.VMEM((2 * LEVELS, WIDTH), jnp.int32),
            pltpu.SMEM((2 * LEVELS, WIDTH), jnp.int32),
            dma((ROWS // GROUP + 1,)),
            dma((2,)),
            pltpu.SemaphoreType.REGULAR,
            dma((2,)),
            dma((2,)),
            dma((ITERS,)),
            dma((ITERS,)),
            dma((ITERS,)),
            dma((2, 2, ITERS)),
            dma((3,)),
            dma((3,)),
            dma((ITERS,)),
            dma((ITERS,)),
            dma((OWNERS,)),
            dma((OWNERS,)),
            dma,
            dma,
        ],
        compiler_params=pltpu.CompilerParams(collective_id=0, has_side_effects=True),
    )(forcing, kappa_lon, kappa_lat, shear, amplitude, tile_owner)


def solution(mesh):
    return jax.shard_map(
        per_device,
        mesh=mesh,
        in_specs=(P(None, "lat", "lon"),) * 5 + (P("lat", "lon"),),
        out_specs=P("lat", "lon", None, None),
        check_vma=False,
    )
```

```python
import functools

import jax
import jax.numpy as jnp
from jax import lax
from jax.experimental import pallas as pl
from jax.experimental.pallas import tpu as pltpu
from jax.sharding import PartitionSpec as P

ITERS = 6
RELAYED = 6
DEEP = ITERS // 2
LEVELS = 8
WIDTH = 128
ROWS = 24
TILES = 4
RING = 5
GROUP = 8
TOTAL = ROWS + 2 * GROUP
OWNERS = 8
MOST = 12
CHIPS_Z = 12
PIECES = 2
MESH = pl.DeviceIdType.MESH


def lanes(shape=(LEVELS, WIDTH)):
    return lax.broadcasted_iota(jnp.int32, shape, len(shape) - 1)


def neighbours(row, lane):
    left = [pltpu.roll(v, WIDTH - 1, axis=1) for v in row]
    right = [pltpu.roll(v, 1, axis=1) for v in row]
    east = [jnp.where(lane == WIDTH - 1, left[(q + 1) % RING], left[q]) for q in range(RING)]
    west = [jnp.where(lane == 0, right[(q - 1) % RING], right[q]) for q in range(RING)]
    both = [e + w for e, w in zip(east, west)]
    slope = [e - w for e, w in zip(east, west)]
    return both, slope


def updated(field, r, south, centre, north, lane_terms, sign):
    south_slope, both, north_slope = lane_terms
    new = []
    for q in range(RING):
        twice = 2.0 * centre[q]
        change = field[r, 1, q] * (both[q] - twice)
        change = change + field[r, 2, q] * (north[q] + south[q] - twice)
        cross = north_slope[q] - south_slope[q]
        change = change + field[r, 3, q] * (cross if sign is None else sign * cross)
        new.append(centre[q] + change)
    return new


def row_of(field, later, turn, r):
    return [field[r, 0, q] if turn == 0 else later[(turn - 1) % 2, r, q] for q in range(RING)]


def store(later, turn, r, new):
    for q in range(RING):
        later[(turn - 1) % 2, r, q] = new[q]


def sweep(field, later, turn, low, count):
    lane = lanes()
    south = row_of(field, later, turn - 1, low - 1)
    centre = row_of(field, later, turn - 1, low)
    _, south_slope = neighbours(south, lane)
    both, slope = neighbours(centre, lane)

    def body(i, carry):
        south, south_slope, centre, both, slope = carry
        r = low + i
        north = row_of(field, later, turn - 1, r + 1)
        north_both, north_slope = neighbours(north, lane)
        store(later, turn, r, updated(field, r, south, centre, north, (south_slope, both, north_slope), None))
        return centre, slope, north, north_both, north_slope

    lax.fori_loop(0, count, body, (south, south_slope, centre, both, slope), unroll=2)


def wedge(field, later, start, step, sign):
    lane = lanes()
    rows = [row_of(field, later, 0, start + step * (j - 1)) for j in range(DEEP)]
    for turn in range(1, ITERS + 1):
        base = start + step * (turn - 1)
        rows = rows + [row_of(field, later, turn - 1, base + step * (DEEP - 1 + j)) for j in range(2)]
        terms = [neighbours(row, lane) for row in rows]
        new = []
        for j in range(DEEP):
            around = (terms[j][1], terms[j + 1][0], terms[j + 2][1])
            new.append(updated(field, base + step * j, rows[j], rows[j + 1], rows[j + 2], around, sign))
        for j in range(DEEP):
            store(later, turn, base + step * j, new[j])
        rows = new


def kernel(
    forcing, kappa_lon, kappa_lat, shear, amplitude, owner, out,
    raw, field, later, scale, stage, lon_send, lon_recv, lat_recv, packed, owner_s, index_v, index_s,
    load_sem, owner_sem, ready_sem, lon_ssem, lon_rsem, north_ssem, relay_ssem, south_ssem, lat_rsem,
    ends_ssem, ends_rsem, stage_rsem, forward_ssem, out_ssem, out_rsem, own_sem, index_sem,
):
    s = lax.axis_index("lon")
    a = lax.axis_index("lat")
    n_lon = lax.axis_size("lon")
    n_lat = lax.axis_size("lat")
    along = lax.rem(a, CHIPS_Z)
    fold = a // (n_lat - 1)
    has_south = (a + n_lat - 1) // n_lat
    wrap = along // (CHIPS_Z - 1) * (1 - fold)
    far = (CHIPS_Z - 1 - along) // (CHIPS_Z - 1) * has_south
    near = has_south - far
    relay_north = ((along == CHIPS_Z - 2) & (a >= CHIPS_Z)).astype(jnp.int32)
    yields = (a == n_lat - CHIPS_Z).astype(jnp.int32)
    relay_south = ((along == 1) & (a < n_lat - CHIPS_Z)).astype(jnp.int32)
    north_lon = s + fold * (n_lon - 1 - 2 * s)
    north_lat = a + 1 - fold
    east = lax.rem(s + 1, n_lon)
    west = lax.rem(s + n_lon - 1, n_lon)
    groups = ROWS // GROUP
    top = GROUP + ROWS
    lane = lanes()
    fields = (forcing, kappa_lon, kappa_lat, shear, amplitude)

    def load(g, i, q, sem):
        cells = pl.ds(q * WIDTH, WIDTH)
        return pltpu.make_async_copy(fields[i].at[:, pl.ds(g * GROUP, GROUP), cells], raw.at[g, i, q], sem)

    def load_group(g):
        for i in range(4):
            for q in range(TILES):
                load(g, i, q, load_sem.at[g]).start()

    owner_copy = pltpu.make_async_copy(owner, owner_s, owner_sem.at[0])
    load_group(groups - 1)
    owner_copy.start()

    barrier = pltpu.get_barrier_semaphore()

    def enter(condition, lon, lat):
        @pl.when(condition == 1)
        def _():
            pl.semaphore_signal(barrier, inc=1, device_id=(lon, lat), device_id_type=MESH)

    for side_lon in (west, s, east):
        enter(1 - fold - wrap, side_lon, a + 1)
        enter(has_south, side_lon, a - 1)
    enter(far, s, a + CHIPS_Z - 2)
    enter(relay_south, s, a + CHIPS_Z - 1)
    enter(relay_south, s, a + CHIPS_Z - 2)
    enter(relay_north, s, a - (CHIPS_Z - 1))
    for d in range(1, OWNERS):
        pl.semaphore_signal(barrier, inc=1, device_id=(lax.rem(s + d, n_lon), a), device_id_type=MESH)

    load_group(0)

    flat = raw.reshape(groups * 5 * TILES * LEVELS * GROUP, WIDTH)

    def cells_of(g, i, q, rr):
        return flat[pl.ds(((g * 5 + i) * TILES + q) * LEVELS * GROUP + rr, LEVELS, GROUP)]

    def prepare_group(g):
        whole = raw.at[g, pl.ds(0, 4)]
        pltpu.make_async_copy(whole, whole, load_sem.at[g]).wait()

        def prepare(rr, _):
            r = g * GROUP + rr
            for q in range(TILES):
                sea = (owner_s[q, r] >= 0).astype(jnp.float32)
                k_lon = cells_of(g, 1, q, rr)
                k_lat = cells_of(g, 2, q, rr)
                cross = 0.5 * cells_of(g, 3, q, rr) * jnp.sqrt(k_lon * k_lat)
                field[GROUP + r, 0, q] = sea * cells_of(g, 0, q, rr)
                field[GROUP + r, 1, q] = sea * k_lon
                field[GROUP + r, 2, q] = sea * k_lat
                field[GROUP + r, 3, q] = sea * cross
            return 0

        lax.fori_loop(0, GROUP, prepare, 0)

    def remote(src, dst, ssem, rsem, lon, lat):
        return pltpu.make_async_remote_copy(
            src_ref=src, dst_ref=dst, send_sem=ssem, recv_sem=rsem, device_id=(lon, lat), device_id_type=MESH
        )

    def part(ref, place, k, first=0, count=TILES):
        return ref.at[place, pl.ds(0, 4 if k < ITERS else 1), pl.ds(first, count)]

    half = TILES // 2

    def north_copies(k_size, k):
        own = top - k
        plain = remote(
            part(field, own, k_size), part(field, GROUP - k + fold * (top - 1 - GROUP + 2 * k), k_size),
            north_ssem.at[k - 1], lat_rsem.at[fold, 0, k - 1], north_lon, north_lat,
        )
        direct = remote(
            part(field, own, k_size, 0, half), part(field, GROUP - k, k_size, 0, half),
            north_ssem.at[k - 1], lat_rsem.at[0, 0, k - 1], s, north_lat,
        )
        around = remote(
            part(field, own, k_size, half, half), part(stage, k - 1, k_size, half, half),
            relay_ssem.at[k - 1], stage_rsem.at[k - 1], s, lax.rem(a + CHIPS_Z - 1, n_lat),
        )
        return plain, direct, around

    def south_copies(k_size, k):
        own = GROUP + k - 1
        plain = remote(
            part(field, own, k_size), part(field, top + k - 1, k_size),
            south_ssem.at[k - 1], lat_rsem.at[1, 0, k - 1], s, lax.rem(a + n_lat - 1, n_lat),
        )
        direct = remote(
            part(field, own, k_size, 0, half), part(field, top + k - 1, k_size, 0, half),
            south_ssem.at[k - 1], lat_rsem.at[1, 0, k - 1], s, lax.rem(a + n_lat - 1, n_lat),
        )
        around = remote(
            part(field, own, k_size, half, half), part(stage, k - 1, k_size, half, half),
            relay_ssem.at[k - 1], stage_rsem.at[k - 1], s, lax.rem(a + n_lat - (CHIPS_Z - 1), n_lat),
        )
        return plain, direct, around

    def each_row(low, high, act):
        for_size = min(high, ITERS - 1)

        def one(k, _):
            act(1, k)
            return 0

        lax.fori_loop(low, for_size + 1, one, 0)
        if high == ITERS:
            act(ITERS, ITERS)

    def send_north(low, high):
        def act(k_size, k):
            plain, direct, around = north_copies(k_size, k)
            split = (wrap == 1) & (k <= RELAYED)

            @pl.when(~split)
            def _():
                plain.start()

            @pl.when(split)
            def _():
                direct.start()
                around.start()

        each_row(low, high, act)

    def send_south(near_or_far):
        for j in range(2):
            ends_copy("south", j).start()
        each_row(1, ITERS, lambda k_size, k: south_copies(k_size, k)[near_or_far].start())

    ends_mirrored = remote(
        lon_recv.at[groups - 1], lat_recv.at[1], ends_ssem.at[0, 0], ends_rsem.at[1, 0], north_lon, north_lat
    )
    south_lat = lax.rem(a + n_lat - 1, n_lat)

    def ends_copy(kind, j):
        lon = (west, east)[j]
        if kind == "north":
            return remote(
                lon_send.at[j, groups - 1], lat_recv.at[0, j], ends_ssem.at[0, j], ends_rsem.at[0, j], lon, north_lat
            )
        return remote(lon_send.at[j, 0], lat_recv.at[1, j], ends_ssem.at[1, j], ends_rsem.at[1, j], lon, south_lat)

    to_west = remote(lon_send.at[0], lon_recv.at[:, 0], lon_ssem.at[0], lon_rsem.at[0], west, a)
    to_east = remote(lon_send.at[1], lon_recv.at[:, 1], lon_ssem.at[1], lon_rsem.at[1], east, a)
    early = 4

    owner_copy.wait()
    prepare_group(groups - 1)
    pl.semaphore_wait(barrier, OWNERS - 1 + 3 * (1 - fold) + 3 * near + 2 * wrap + far + relay_north)

    @pl.when(wrap == 1)
    def _():
        for side_lon in (west, s, east):
            pl.semaphore_signal(ready_sem, inc=1, device_id=(side_lon, a + 1), device_id_type=MESH)
        pl.semaphore_signal(ready_sem, inc=1, device_id=(s, a - (CHIPS_Z - 2)), device_id_type=MESH)

    per_vector = WIDTH // GROUP

    def pack_group(g):
        for v in range(PIECES):
            to_west_v = jnp.zeros((LEVELS, WIDTH), jnp.float32)
            to_east_v = jnp.zeros((LEVELS, WIDTH), jnp.float32)
            for j in range(per_vector):
                rr, kind = divmod(v * per_vector + j, 4)
                r = GROUP + g * GROUP + rr
                here = lane // GROUP == j
                first, last = field[r, kind, 0], field[r, kind, TILES - 1]
                if j:
                    first = pltpu.roll(first, GROUP * j, axis=1)
                if j < per_vector - 1:
                    last = pltpu.roll(last, GROUP * (j + 1), axis=1)
                to_west_v = jnp.where(here, first, to_west_v)
                to_east_v = jnp.where(here, last, to_east_v)
            lon_send[0, g, v] = to_west_v
            lon_send[1, g, v] = to_east_v

    @pl.when(fold == 0)
    def _():
        send_north(1, early)

    pack_group(groups - 1)

    @pl.when(fold == 0)
    def _():
        for j in range(2):
            ends_copy("north", j).start()

    load_group(1)
    prepare_group(0)
    pack_group(0)
    for g in range(groups):
        for q in range(TILES):
            load(g, 4, q, load_sem.at[groups]).start()
    prepare_group(1)
    pack_group(1)
    to_west.start()
    to_east.start()

    @pl.when(fold == 0)
    def _():
        send_north(early + 1, ITERS)

    @pl.when(fold == 1)
    def _():
        send_north(1, ITERS)

    @pl.when(near == 1)
    def _():
        send_south(0)

    @pl.when(far == 1)
    def _():
        each_row(1, ITERS, lambda k_size, k: south_copies(k_size, k)[2].start())

    def unpack(buf, g, base, step):
        for v in range(PIECES):
            from_east, from_west = buf[g, 0, v], buf[g, 1, v]
            for j in range(per_vector):
                rr, kind = divmod(v * per_vector + j, 4)
                after = from_east if j == 0 else pltpu.roll(from_east, WIDTH - GROUP * j, axis=1)
                before = from_west if j == per_vector - 1 else pltpu.roll(from_west, WIDTH - GROUP * (j + 1), axis=1)
                ends = jnp.where(lane < ITERS, after, jnp.where(lane >= WIDTH - ITERS, before, 0.0))
                field[base + step * rr, kind, TILES] = ends

    amplitudes = raw.at[:, pl.ds(4, 1)]
    pltpu.make_async_copy(amplitudes, amplitudes, load_sem.at[groups]).wait()

    def scale_group(g, _):
        def scale_row(rr, _):
            for q in range(TILES):
                scale[g * GROUP + rr, q] = cells_of(g, 4, q, rr)
            return 0

        return lax.fori_loop(0, GROUP, scale_row, 0)

    lax.fori_loop(0, groups, scale_group, 0)

    down = lax.broadcasted_iota(jnp.int32, (LEVELS, WIDTH), 0)
    column = lax.rem(lane, TILES)
    carried = jnp.zeros((1, WIDTH), jnp.int32)
    ranks, numbers = [], []
    for g in range(groups):
        spread = jnp.full((GROUP, WIDTH), -1, jnp.int32)
        for rr in range(GROUP):
            for q in range(TILES):
                spread = jnp.where((down == rr) & (column == q), owner_s[q, g * GROUP + rr], spread)
        mine = (spread == lane // TILES).astype(jnp.int32)
        within = mine + jnp.where(column >= 1, pltpu.roll(mine, 1, axis=1), 0)
        within = within + jnp.where(column >= 2, pltpu.roll(within, 2, axis=1), 0)
        total = mine + jnp.where(column % 2 == 0, pltpu.roll(mine, WIDTH - 1, axis=1), pltpu.roll(mine, 1, axis=1))
        total = total + jnp.where(column < 2, pltpu.roll(total, WIDTH - 2, axis=1), pltpu.roll(total, 2, axis=1))
        upto = total
        for shift in (1, 2, 4):
            upto = upto + jnp.where(down >= shift, pltpu.roll(upto, shift, axis=0), 0)
        ranks.append(jnp.where(mine == 1, carried + upto - total + within, 0))
        numbers.append((g * GROUP + down) * TILES + column + 1)
        carried = carried + jnp.sum(total, axis=0, keepdims=True)
    for k in range(MOST):
        place = jnp.zeros((LEVELS, WIDTH), jnp.int32)
        for g in range(groups):
            place = place + jnp.where(ranks[g] == k + 1, numbers[g], 0)
        place = jnp.sum(place, axis=0, keepdims=True)
        place = place + pltpu.roll(jnp.broadcast_to(place, (LEVELS, WIDTH)), WIDTH - 1, axis=1)
        place = place + pltpu.roll(place, WIDTH - 2, axis=1)
        index_v[k : k + 1, :] = place[0:1, :] - 1
    index_copy = pltpu.make_async_copy(index_v, index_s, index_sem)
    index_copy.start()

    to_west.wait_recv()
    to_east.wait_recv()

    @pl.when(fold == 1)
    def _():
        ends_mirrored.start()

    def unpack_own(g, _):
        unpack(lon_recv, g, GROUP + g * GROUP, 1)
        return 0

    lax.fori_loop(0, groups, unpack_own, 0)

    def relay_copies(k_size, k):
        north = remote(
            part(stage, k - 1, k_size, half, half), part(field, GROUP - k, k_size, half, half),
            forward_ssem.at[k - 1], lat_rsem.at[0, 1, k - 1], s, lax.rem(a + n_lat - (CHIPS_Z - 2), n_lat),
        )
        south = remote(
            part(stage, k - 1, k_size, half, half), part(field, top + k - 1, k_size, half, half),
            forward_ssem.at[k - 1], lat_rsem.at[1, 1, k - 1], s, lax.rem(a + CHIPS_Z - 2, n_lat),
        )
        return north, south

    for turn in range(1, ITERS + 1):
        sweep(field, later, turn, GROUP + turn, ROWS - 2 * turn)

        @pl.when(relay_north == 1)
        def _():
            north_copies(turn, turn)[2].wait_recv()
            relay_copies(turn, turn)[0].start()

    def clear(r, _):
        zero = jnp.zeros((LEVELS, WIDTH), jnp.float32)
        for kind in range(4):
            for q in range(RING):
                field[r, kind, q] = zero
        return 0

    def mirrored(value):
        return jnp.take_along_axis(value, WIDTH - 1 - lane, axis=1)

    def mirror_ends(i, _):
        for kind in range(4):
            field[top + i, kind, TILES] = mirrored(field[top + i, kind, TILES])
        return 0

    def mirror_row(r):
        for kind in range(4):
            old = [field[r, kind, q] for q in range(TILES)]
            for q in range(TILES):
                field[r, kind, q] = mirrored(old[TILES - 1 - q])

    late = wrap + fold

    def edge(i, _):
        side = lax.rem(i + 1 - late, 2)
        step = 1 - 2 * side
        sign = step.astype(jnp.float32)
        arrives = (side + has_south + 1) // 2
        mirror = side * fold
        halves = (1 - side) * far

        @pl.when(halves - yields == 1)
        def _():
            pl.semaphore_wait(ready_sem, 3)
            send_south(1)

        whole = side * fold

        @pl.when(whole == 1)
        def _():
            remote(lon_recv.at[0], lat_recv.at[side], ends_ssem.at[0, 0], ends_rsem.at[side, 0], s, south_lat).wait_recv()

        @pl.when(arrives - whole == 1)
        def _():
            for j in range(2):
                remote(
                    lon_send.at[j, 0], lat_recv.at[side, j], ends_ssem.at[0, j], ends_rsem.at[side, j], s, south_lat
                ).wait_recv()

        @pl.when(arrives == 1)
        def _():
            unpack(lat_recv, side, side * top + mirror * (GROUP - 1), 1 - 2 * mirror)

        @pl.when(mirror == 1)
        def _():
            lax.fori_loop(0, GROUP, mirror_ends, 0)

        @pl.when(arrives == 0)
        def _():
            lax.fori_loop(0, GROUP, clear, 0)

        def arrive(k_size, k):
            def await_row(part_of, first, count):
                place = part(field, GROUP, k_size, first, count)
                remote(
                    place, place, north_ssem.at[k - 1], lat_rsem.at[side, part_of, k - 1], north_lon, north_lat
                ).wait_recv()

            split = ((halves == 1) & (k <= RELAYED)) | (side * wrap == 1)

            @pl.when((arrives == 1) & ~split)
            def _():
                await_row(0, 0, TILES)

            @pl.when(split)
            def _():
                await_row(0, 0, half)
                await_row(1, half, half)

            @pl.when(mirror == 1)
            def _():
                mirror_row(top + k - 1)

        def outward(h, _):
            def one(j, _):
                arrive(1, h * DEEP + j)
                return 0

            lax.fori_loop(1, DEEP, one, 0)

            @pl.when(h == 0)
            def _():
                arrive(1, DEEP)

            @pl.when(h == 1)
            def _():
                arrive(ITERS, ITERS)

            wedge(field, later, GROUP + side * (ROWS - 1) + step * (1 - DEEP * (h + 1)), step, sign)
            return 0

        lax.fori_loop(0, 2, outward, 0)
        return 0

    lax.fori_loop(0, 2, edge, 0)

    index_copy.wait()

    def fill(o):
        for k in range(MOST):
            t = index_s[k, o * TILES]
            r = jnp.maximum(t, 0) // TILES
            q = jnp.maximum(t, 0) - r * TILES
            tile = scale[r, q] * later[(ITERS - 1) % 2, GROUP + r, q]
            packed[o * MOST + k] = jnp.where(t >= 0, tile, 0.0)

    def to_owner(o, d):
        block = pl.ds(o * MOST, MOST)
        slot = pl.ds(s * MOST, MOST)
        return remote(packed.at[block], out.at[0, slot], out_ssem.at[d], out_rsem.at[d], o, a)

    part_lon = n_lon // 2

    def give(i, _):
        other = (s // part_lon + 1 + i // part_lon) % 2
        o = other * part_lon + lax.rem(s + i, part_lon)

        @pl.when(i != part_lon)
        def _():
            fill(o)
            to_owner(o, lax.rem(o + n_lon - s, n_lon)).start()

        return 0

    lax.fori_loop(0, OWNERS, give, 0)

    @pl.when(yields == 1)
    def _():
        pl.semaphore_wait(ready_sem, 3)
        send_south(1)

    fill(s)
    own = pltpu.make_async_copy(packed.at[pl.ds(s * MOST, MOST)], out.at[0, pl.ds(s * MOST, MOST)], own_sem)
    own.start()
    @pl.when(relay_south == 1)
    def _():
        pl.semaphore_wait(ready_sem, 1)

        def act(k_size, k):
            south_copies(k_size, k)[2].wait_recv()
            relay_copies(k_size, k)[1].start()

        each_row(1, ITERS, act)

    to_west.wait_send()
    to_east.wait_send()

    @pl.when(fold == 0)
    def _():
        for j in range(2):
            ends_copy("north", j).wait_send()

    @pl.when(fold == 1)
    def _():
        ends_mirrored.wait_send()

    def drain(k_size, k):
        plain, direct, around = north_copies(k_size, k)
        split = (wrap == 1) & (k <= RELAYED)

        @pl.when(~split)
        def _():
            plain.wait_send()

        @pl.when(split)
        def _():
            direct.wait_send()
            around.wait_send()

        @pl.when(near == 1)
        def _():
            south_copies(k_size, k)[0].wait_send()

        @pl.when(far == 1)
        def _():
            south_copies(k_size, k)[1].wait_send()
            south_copies(k_size, k)[2].wait_send()

        @pl.when(relay_south == 1)
        def _():
            relay_copies(k_size, k)[1].wait_send()

        @pl.when((relay_north == 1) & (k <= RELAYED))
        def _():
            relay_copies(k_size, k)[0].wait_send()

    each_row(1, ITERS, drain)

    @pl.when(has_south == 1)
    def _():
        for j in range(2):
            ends_copy("south", j).wait_send()

    own.wait()

    def finish(d, _):
        to_owner(lax.rem(s + d, n_lon), d).wait()
        return 0

    lax.fori_loop(1, OWNERS, finish, 0)


def per_device(forcing, kappa_lon, kappa_lat, shear, amplitude, tile_owner):
    vmem = functools.partial(pltpu.VMEM, dtype=jnp.float32)
    dma = pltpu.SemaphoreType.DMA
    return pl.pallas_call(
        kernel,
        out_shape=jax.ShapeDtypeStruct((1, OWNERS * MOST, LEVELS, WIDTH), jnp.float32),
        in_specs=[pl.BlockSpec(memory_space=pl.ANY)] * 6,
        out_specs=pl.BlockSpec(memory_space=pl.ANY),
        scratch_shapes=[
            vmem((ROWS // GROUP, 5, TILES, LEVELS, GROUP, WIDTH)),
            vmem((TOTAL, 4, RING, LEVELS, WIDTH)),
            vmem((2, TOTAL, RING, LEVELS, WIDTH)),
            vmem((ROWS, TILES, LEVELS, WIDTH)),
            vmem((ITERS, 4, TILES, LEVELS, WIDTH)),
            vmem((2, ROWS // GROUP, PIECES, LEVELS, WIDTH)),
            vmem((ROWS // GROUP, 2, PIECES, LEVELS, WIDTH)),
            vmem((2, 2, PIECES, LEVELS, WIDTH)),
            vmem((OWNERS * MOST, LEVELS, WIDTH)),
            pltpu.SMEM((TILES, ROWS), jnp.int32),
            pltpu.VMEM((2 * LEVELS, WIDTH), jnp.int32),
            pltpu.SMEM((2 * LEVELS, WIDTH), jnp.int32),
            dma((ROWS // GROUP + 1,)),
            dma((1,)),
            pltpu.SemaphoreType.REGULAR,
            dma((2,)),
            dma((2,)),
            dma((ITERS,)),
            dma((ITERS,)),
            dma((ITERS,)),
            dma((2, 2, ITERS)),
            dma((3, 2)),
            dma((3, 2)),
            dma((ITERS,)),
            dma((ITERS,)),
            dma((OWNERS,)),
            dma((OWNERS,)),
            dma,
            dma,
        ],
        compiler_params=pltpu.CompilerParams(collective_id=0, has_side_effects=True),
    )(forcing, kappa_lon, kappa_lat, shear, amplitude, tile_owner.T)


def solution(mesh):
    return jax.shard_map(
        per_device,
        mesh=mesh,
        in_specs=(P(None, "lat", "lon"),) * 5 + (P("lat", "lon"),),
        out_specs=P("lat", "lon", None, None),
        check_vma=False,
    )
```
